256 devices in a mesh: dp: 4 (over x), expert: 64 (over z, y, core).
Axes of the slice: x: 4, y: 4, z: 8, core: 2. Of those that a mesh axis runs over, the one named last changes fastest.
Arguments:
- hidden_in: bfloat16 [32768, 2048], P(('dp', 'expert')), may hold values from -6 to 6
- queries: bfloat16 [32768, 2048], P(('dp', 'expert')), may hold values from -150 to 150, as said below
- keys_values: bfloat16 [32768, 512], P(('dp', 'expert')), may hold values from -5 to 5
- segment_ids: int32 [4, 8192], P('dp', 'expert'), may hold values from 0 to 7, never falling along the last dimension, each value on 1 to 4096 neighbouring positions
- routes: int32 [32768, 8], P(('dp', 'expert')), may hold values from 0 to 63, all different within a row; in each aligned block of 128 rows (0 to 127, 128 to 255, ...) at most 24 rows name the same one
- gate_weights: float32 [32768, 8], P(('dp', 'expert')), may hold values from 0.05 to 1
- page_table: int32 [4, 512], P('dp'), may hold values from 0 to 511, each once within a row
- out_weight: bfloat16 [2048, 2048], P('dp'), may hold values from -0.125 to 0.125
- norm_gain: float32 [2048], replicated, may hold values from 0.1 to 1.9
- expert_gate: bfloat16 [64, 2048, 384], P('expert'), may hold values from -0.125 to 0.125
- expert_up: bfloat16 [64, 2048, 384], P('expert'), may hold values from -0.125 to 0.125
- expert_down: bfloat16 [64, 384, 2048], P('expert'), may hold values from -0.3125 to 0.3125
Outputs:
- hidden_out: bfloat16 [32768, 2048], P(('dp', 'expert'))
- cache_pages: bfloat16 [2048, 16, 512], P(('dp', 'expert'))
The draws below stay inside these ranges and needn't reach their ends.
Inputs may be any that keep to these rules, and one draw needn't show every extreme that they name: `queries`: queries (hidden draw: some equal a multiple of their own key). `segment_ids`: within a pack numbers never fall; each prompt has 1 to 4096 tokens and some prompt has exactly 4096. `routes`: each row names 8 different experts; among the rows of one device no expert is named more than 24 times, a bound that some block reaches. `page_table`: each row is a permutation of its pack's 512 slots.
All inputs are finite; a program needn't handle non-finite values.
Results may differ from the reference program's by a relative error of at most 0.007.
Values may be sent and summed in bfloat16 or wider, within the bound.
A program may use at most 128 MiB of HBM per device.

```python
import math
import jax
import jax.numpy as jnp
import numpy as np
from jax import lax

D = 2048
HD = 128
HQ = 16
HK = 2
FW = 384
TOP = 8
PAGE = 16
DOCS = 8
TOK_DEV = 128
EXPERTS = 64
PACK = 8192
TOKENS = 32768
MOST_LEN = 4096
PAGES = 512
CAP = 24
N_DP = 4
N_EXPERT = 64


def paired_draw(key):
    base_key = jax.random.fold_in(key, 1301)
    key_q, key_kv = jax.random.split(base_key, 2)
    queries = jnp.clip(jax.random.normal(key_q, (TOKENS, HQ * HD), jnp.float32), -6.0, 6.0)
    keys_values = jnp.clip(jax.random.normal(key_kv, (TOKENS, 2 * HK * HD), jnp.float32), -5.0, 5.0)
    return (queries, keys_values)


def draw_queries(key, part):
    return paired_draw(key)[0].astype(jnp.bfloat16)


def draw_keys_values(key, part):
    return paired_draw(key)[1].astype(jnp.bfloat16)


def block_levels(rng, extent, cuts, least, largest):
    def one(position, blocks):
        steps = jax.random.uniform(jax.random.fold_in(jax.random.fold_in(rng, 6), position), (blocks,), jnp.float32, least / len(cuts), largest / len(cuts))
        return jnp.repeat(jnp.exp(steps), extent[position] // blocks).reshape((-1,) + (1,) * (len(extent) - position - 1))

    loudness = one(*cuts[0])
    for cut in cuts[1:]:
        loudness = loudness * one(*cut)
    return loudness


def length_profile(amount, total, reach, slope):
    weights = [(1 << 20) // math.isqrt(standing ** slope) + 1 for standing in range(2, amount + 1)]
    rest, counts = total - reach - (amount - 1), [1] * (amount - 1)
    while rest > 0:
        free = [i for i in range(amount - 1) if counts[i] < reach]
        whole, remaining = sum([weights[i] for i in free]), rest
        for i in free:
            extra = min(reach - counts[i], max(1, remaining * weights[i] // whole), rest)
            counts[i] = counts[i] + extra
            rest = rest - extra
    return np.array([reach] + counts)


def ragged_sizes(own_key, count, total, bound, lean):
    if count == 2:
        one = jax.random.randint(own_key, (), max(1, total - bound), min(bound, total - 1) + 1)
        return jnp.stack([one, total - one])
    lengths = jnp.asarray(length_profile(count, total, bound, lean), jnp.int32)
    pairs = (count - 1) // 2
    donor, sink = lengths[1:1 + 2 * pairs:2], lengths[2:2 + 2 * pairs:2]
    room = jnp.minimum(donor - 1, bound - sink)
    moved = jax.random.randint(jax.random.fold_in(own_key, 1), (pairs,), 0, 1 << 20) % (room + 1)
    lengths = lengths.at[1:1 + 2 * pairs:2].set(donor - moved).at[2:2 + 2 * pairs:2].set(sink + moved)
    return lengths[jax.random.permutation(jax.random.fold_in(own_key, 2), count)]


def routed_block(rng, own, number, rows, count, top, bound, lean):
    sequence = jax.random.permutation(rng, count)
    packed, ordinary = load_shares(count, rows * top, bound, lean, True), load_shares(count, rows * top, bound, lean, False)
    places = jnp.arange(count)

    def named(lengths, offset_by):
        used = int((lengths > 0).sum())
        fixed = max(1, used // 4)
        moved = fixed + (places - fixed + offset_by * (used - fixed)) % max(1, count - fixed)
        return jnp.zeros((count,), jnp.int32).at[sequence[jnp.where(places < fixed, places, moved)]].set(jnp.asarray(lengths, jnp.int32))

    lengths = jnp.where(number % 4 == 0, named(packed, number // 4), named(ordinary, number - number // 4 - 1))
    mixed = jax.random.permutation(jax.random.fold_in(own, 3), count)
    giver, sink = mixed[0:count // 2 * 2:2], mixed[1:count // 2 * 2:2]
    margin = jnp.minimum(lengths[giver] - 1, bound - lengths[sink]) // 2
    margin = jnp.where((giver == sequence[0]) | (sink == sequence[0]) | (lengths[sink] == 0), 0, jnp.maximum(margin, 0))
    moved = jax.random.randint(jax.random.fold_in(own, 4), (count // 2,), 0, 1 << 20) % (margin + 1)
    lengths = lengths.at[giver].add(-moved).at[sink].add(moved)
    members = jnp.searchsorted(jnp.cumsum(lengths), jnp.arange(rows * top), side="right").astype(jnp.int32)
    table = members.reshape(top, rows).T
    table = table[jax.random.permutation(jax.random.fold_in(own, 1), rows)]
    offset_by = jax.random.randint(jax.random.fold_in(own, 2), (rows, 1), 0, top)
    return jnp.take_along_axis(table, (jnp.arange(top)[None, :] + offset_by) % top, axis=1)


def load_shares(amount, total, limit, slope, full):
    portions = [(1 << 20) // math.isqrt(grade ** slope) + 1 for grade in range(1, amount + 1)]
    largest = limit if full else min(limit, max(-(-total // amount), total * portions[0] // sum(portions)))
    least = 1 if total - largest >= amount - 1 else 0
    given, spare = [largest] + [least] * (amount - 1), total - largest - least * (amount - 1)
    while spare > 0:
        candidates = [i for i in range(1, amount) if given[i] < largest] or [i for i in range(1, amount) if given[i] < limit]
        pool, remaining = sum([portions[i] for i in candidates]), spare
        for i in candidates:
            addition = min(limit - given[i], max(1, remaining * portions[i] // pool), spare)
            given[i] = given[i] + addition
            spare = spare - addition
    return np.array(given)


def normal_values(stream_key, extent, width, limit, cuts=(), kind=jnp.bfloat16):
    drawn = jax.random.normal(stream_key, extent, jnp.float32) * width
    if len(cuts) > 0:
        drawn = block_levels(stream_key, extent, cuts, -0.22, 0.18) * drawn
    return jnp.clip(drawn, min=-limit, max=limit).astype(kind)


def setup_inputs(seed: int = 0) -> dict:
    splits = jax.random.split(jax.random.key(seed), 13)
    hidden_in = normal_values(splits[0], (TOKENS, D), 1.0, 6.0, ((0, 256),))
    queries = draw_queries(jax.random.fold_in(splits[12], 71), 0)
    keys_values = draw_keys_values(jax.random.fold_in(splits[12], 71), 0)
    segment_ids = jax.vmap(lambda own: jnp.searchsorted(jnp.cumsum(ragged_sizes(own, DOCS, PACK, MOST_LEN, 2)), jnp.arange(PACK), side="right"))(jax.random.split(splits[3], N_DP)).reshape((N_DP, PACK)).astype(jnp.int32)
    routes_keys = jax.random.split(jax.random.fold_in(splits[4], 1), TOKENS // TOK_DEV)
    routes_turns = jax.random.permutation(jax.random.fold_in(splits[4], 3), TOKENS // TOK_DEV)
    routes = jax.vmap(lambda own, number: routed_block(jax.random.fold_in(splits[4], 2), own, number, TOK_DEV, EXPERTS, TOP, CAP, 2))(routes_keys, routes_turns).reshape((TOKENS, TOP))
    gate_weights = jnp.clip(jnp.exp(math.log(1.0) - 2.9957323 * jax.random.uniform(splits[5], (TOKENS, TOP), jnp.float32) ** block_levels(splits[5], (TOKENS, TOP), ((0, 256),), -0.2, 0.2)), 0.05, 1.0)
    page_table = jax.vmap(lambda own: jax.random.permutation(own, PAGES))(jax.random.split(splits[6], N_DP)).reshape((N_DP, PAGES)).astype(jnp.int32)
    out_weight = normal_values(splits[7], (HQ * HD, D), (HQ * HD) ** -0.5, 0.125, ((0, 4),))
    norm_gain = jnp.clip(1.0 + 0.18 * jax.random.normal(splits[8], (D,), jnp.float32), 0.1, 1.9)
    expert_gate = normal_values(splits[9], (EXPERTS, D, FW), D ** -0.5, 0.125, ((0, 64),))
    expert_up = normal_values(splits[10], (EXPERTS, D, FW), D ** -0.5, 0.125, ((0, 64),))
    expert_down = normal_values(splits[11], (EXPERTS, FW, D), FW ** -0.5, 0.3125, ((0, 64),))
    return {"hidden_in": hidden_in, "queries": queries, "keys_values": keys_values, "segment_ids": segment_ids, "routes": routes, "gate_weights": gate_weights, "page_table": page_table, "out_weight": out_weight, "norm_gain": norm_gain, "expert_gate": expert_gate, "expert_up": expert_up, "expert_down": expert_down}


def reference(hidden_in, queries, keys_values, segment_ids, routes, gate_weights, page_table, out_weight, norm_gain, expert_gate, expert_up, expert_down):
    groups = HQ // HK
    kv_width = HK * HD
    packs_q = queries.reshape(N_DP, PACK, HK, groups, HD)
    packs_kv = keys_values.reshape(N_DP, PACK, 2 * kv_width)
    q_block = min(PACK, 512)
    block_total = PACK // q_block
    positions = jnp.arange(PACK, dtype=jnp.int32)

    def attend(index):
        pack_index = index // block_total
        first_row = index % block_total * q_block
        query_rows = lax.dynamic_slice_in_dim(packs_q[pack_index], first_row, q_block, 0).astype(jnp.float32)
        kv_rows = packs_kv[pack_index]
        key_rows = kv_rows[:, :kv_width].reshape(PACK, HK, HD).astype(jnp.float32)
        value_rows = kv_rows[:, kv_width:].reshape(PACK, HK, HD).astype(jnp.float32)
        segments_row = segment_ids[pack_index]
        query_seg = lax.dynamic_slice_in_dim(segments_row, first_row, q_block, 0)
        query_pos = first_row + jnp.arange(q_block, dtype=jnp.int32)
        allowed = (positions[None, :] <= query_pos[:, None]) & (segments_row[None, :] == query_seg[:, None])
        scores = jnp.einsum('thgd,shd->thgs', query_rows, key_rows) * (1.0 / math.sqrt(HD))
        masked = jnp.where(allowed[:, None, None, :], scores, -1e+30)
        row_top = lax.optimization_barrier(jnp.max(masked, axis=3, keepdims=True))
        probabilities = jnp.where(allowed[:, None, None, :], jnp.exp(masked - row_top), 0.0)
        denominator = lax.optimization_barrier(jnp.sum(probabilities, axis=3))
        rounded = lax.optimization_barrier(probabilities.astype(jnp.bfloat16)).astype(jnp.float32)
        heads_out = jnp.einsum('thgs,shd->thgd', rounded, value_rows) / denominator[..., None]
        return heads_out.reshape(q_block, HQ * HD).astype(jnp.bfloat16)
    attended = lax.map(attend, jnp.arange(N_DP * block_total, dtype=jnp.int32)).reshape(TOKENS, HQ * HD)
    projected = jnp.dot(attended, out_weight, preferred_element_type=jnp.float32)
    residual = hidden_in.astype(jnp.float32) + projected
    normed = (residual * lax.rsqrt(lax.optimization_barrier(jnp.mean(residual * residual, axis=1, keepdims=True)) + 1e-06) * norm_gain).astype(jnp.bfloat16)
    shares = gate_weights / lax.optimization_barrier(jnp.sum(gate_weights, axis=1, keepdims=True))
    row_limit = N_DP * N_EXPERT * CAP

    def per_expert(running, expert):
        chosen = routes == expert
        weight = lax.optimization_barrier(jnp.sum(jnp.where(chosen, shares, 0.0), axis=1))
        routed = jnp.any(chosen, axis=1)
        row_index = jnp.nonzero(routed, size=row_limit, fill_value=0)[0].astype(jnp.int32)
        filled = jnp.arange(row_limit, dtype=jnp.int32) < jnp.sum(routed.astype(jnp.int32))
        inputs = normed[row_index]
        gate_value = jnp.dot(inputs, expert_gate[expert], preferred_element_type=jnp.float32)
        up_value = jnp.dot(inputs, expert_up[expert], preferred_element_type=jnp.float32)
        hidden_units = (jax.nn.silu(gate_value) * up_value).astype(jnp.bfloat16)
        result = lax.optimization_barrier(jnp.dot(hidden_units, expert_down[expert], preferred_element_type=jnp.float32).astype(jnp.bfloat16)).astype(jnp.float32)
        scaled = jnp.where(filled, weight[row_index], 0.0)
        return (running.at[row_index].add(result * scaled[:, None]), None)
    combined, _ = lax.scan(per_expert, jnp.zeros((TOKENS, D), jnp.float32), jnp.arange(EXPERTS, dtype=jnp.int32))
    hidden_out = (residual + combined).astype(jnp.bfloat16)
    page_rows = keys_values.reshape(N_DP * PAGES, PAGE, 2 * kv_width)
    slot_index = (page_table + PAGES * jnp.arange(N_DP, dtype=jnp.int32)[:, None]).reshape(-1).astype(jnp.int32)
    cache_pages = jnp.zeros((N_DP * PAGES, PAGE, 2 * kv_width), jnp.bfloat16).at[slot_index].set(page_rows)
    return (hidden_out, cache_pages)
```

```python
import functools
import math

import jax
import jax.numpy as jnp
from jax import lax
from jax.experimental import pallas as pl
from jax.experimental.pallas import tpu as pltpu
from jax.sharding import PartitionSpec as P

HD = 128
HQ = 16
HK = 2
TOP = 8
PAGE = 16

neg_big = -1e30
norm_eps = 1e-06

NZ, NY, NC = 8, 4, 2
PLANE = NY * NC
CAP = 24
VMEM_LIMIT = 64 * 1024 * 1024 - 2 * 1024 * 1024
MESH = pl.DeviceIdType.MESH
ORDER = (0, 1, 2, -2, 3, -3, 4, -1)
SLOT = {d: k for k, d in enumerate(ORDER)}


def pick(table, k):
    if isinstance(k, int):
        return table[k]
    value = jnp.int32(table[0])
    for j in range(1, len(table)):
        value = jnp.where(k == j, jnp.int32(table[j]), value)
    return value


def moe_kernel(
    normed_ref, residual_ref, meta_ref, wg_hbm, wu_hbm, wd_hbm, out_ref,
    x_buf, meta_buf, snd, arr, res, ret, part_out, part_in, acc, w_in, w_down,
    ring_send, ring_recv, meta_send, meta_recv, disp_send, disp_recv, disp_self,
    back_send, back_recv, back_self, part_send, part_recv, weight_sem,
):
    me = lax.axis_index("expert")
    z = me // PLANE
    pos = me % PLANE
    rows, width = normed_ref.shape
    fw = w_down.shape[0]

    def at_z(target):
        return {"expert": lax.rem(target + 2 * NZ, NZ) * PLANE + pos}

    def at_plane(target):
        return {"expert": z * PLANE + target}

    loads = [
        pltpu.make_async_copy(wg_hbm.at[0], w_in.at[:, pl.ds(0, fw)], weight_sem.at[0]),
        pltpu.make_async_copy(wu_hbm.at[0], w_in.at[:, pl.ds(fw, fw)], weight_sem.at[1]),
        pltpu.make_async_copy(wd_hbm.at[0], w_down, weight_sem.at[2]),
    ]
    for load in loads:
        load.start()

    barrier = pltpu.get_barrier_semaphore()
    for d in range(1, NZ):
        pl.semaphore_signal(barrier, inc=1, device_id=at_z(z + d), device_id_type=MESH)
    for o in range(1, PLANE):
        pl.semaphore_signal(
            barrier, inc=1, device_id=at_plane(lax.rem(pos + o, PLANE)), device_id_type=MESH
        )
    pl.semaphore_wait(barrier, NZ - 1 + PLANE - 1)

    def ring_copy(src, slot, sem, toward, first=0, count=None):
        count = rows if count is None else count
        return pltpu.make_async_remote_copy(
            src_ref=src.at[pl.ds(first, count)],
            dst_ref=x_buf.at[slot, pl.ds(first, count)],
            send_sem=ring_send.at[sem],
            recv_sem=ring_recv.at[sem],
            device_id=at_z(z + toward),
            device_id_type=MESH,
        )

    half = rows // 2
    down = [ring_copy(normed_ref, SLOT[1], SLOT[1], -1)]
    up = [ring_copy(normed_ref, SLOT[-1], SLOT[-1], 1)]
    for d in (1, 2):
        down.append(ring_copy(x_buf.at[SLOT[d]], SLOT[d + 1], SLOT[d + 1], -1))
        up.append(ring_copy(x_buf.at[SLOT[-d]], SLOT[-d - 1], SLOT[-d - 1], 1))
    down.append(ring_copy(x_buf.at[SLOT[3]], SLOT[4], SLOT[4], -1, 0, half))
    up.append(ring_copy(x_buf.at[SLOT[-3]], SLOT[4], NZ, 1, half, half))

    down[0].start()
    up[0].start()
    for k in range(1, NZ):
        copy = pltpu.make_async_remote_copy(
            src_ref=meta_ref,
            dst_ref=meta_buf.at[k],
            send_sem=meta_send,
            recv_sem=meta_recv,
            device_id=at_z(z - ORDER[k]),
            device_id_type=MESH,
        )
        copy.start()
    meta_buf[0] = meta_ref[...]

    row_id = lax.broadcasted_iota(jnp.int32, (rows, rows), 0)
    col_id = lax.broadcasted_iota(jnp.int32, (rows, rows), 1)
    earlier = (row_id < col_id).astype(jnp.bfloat16)
    first_expert = z * PLANE
    expert_id = (first_expert + lax.broadcasted_iota(jnp.int32, (PLANE, rows), 0)).astype(
        jnp.float32
    )
    slot_id = lax.broadcasted_iota(jnp.int32, (CAP, rows), 0).astype(jnp.float32)

    def chosen(k, weighted):
        meta = meta_buf[k]
        mask = jnp.zeros((PLANE, rows), jnp.float32)
        share = jnp.zeros((PLANE, rows), jnp.float32)
        for n in range(TOP):
            hit = meta[n : n + 1, :] == expert_id
            mask = jnp.where(hit, 1.0, mask)
            if weighted:
                share = jnp.where(hit, meta[TOP + n : TOP + n + 1, :], share)
        rank = jnp.dot(mask.astype(jnp.bfloat16), earlier, preferred_element_type=jnp.float32)
        rank = jnp.where(mask > 0.5, rank, -1.0)
        value = share if weighted else mask
        pieces = [
            jnp.where(rank[e : e + 1, :] == slot_id, value[e : e + 1, :], 0.0)
            for e in range(PLANE)
        ]
        return jnp.concatenate(pieces, axis=0).astype(jnp.bfloat16)

    def exchange(src, dst, k, send_sem, recv_sem, self_sem):
        copies = []
        for o in range(1, PLANE):
            target = lax.rem(pos + o, PLANE)
            copies.append(
                pltpu.make_async_remote_copy(
                    src_ref=src.at[k, target],
                    dst_ref=dst.at[k, pos],
                    send_sem=send_sem.at[k],
                    recv_sem=recv_sem.at[k],
                    device_id=at_plane(target),
                    device_id_type=MESH,
                )
            )
        own = pltpu.make_async_copy(src.at[k, pos], dst.at[k, pos], self_sem.at[k])
        return copies, own

    def start_exchange(*args):
        copies, own = exchange(*args)
        for copy in copies:
            copy.start()
        own.start()

    def others(buf, k):
        return buf.at[k, pl.ds(0, PLANE - 1)]

    def wait_exchange(src, dst, k, send_sem, recv_sem, self_sem):
        pltpu.make_async_copy(others(dst, k), others(dst, k), recv_sem.at[k]).wait()
        pltpu.make_async_copy(src.at[k, pos], dst.at[k, pos], self_sem.at[k]).wait()

    def wait_sent(src, dst, k, send_sem, recv_sem, self_sem):
        pltpu.make_async_copy(others(src, k), others(src, k), send_sem.at[k]).wait()

    disp = (disp_send, disp_recv, disp_self)
    back = (back_send, back_recv, back_self)

    def part_copy(k):
        return pltpu.make_async_remote_copy(
            src_ref=part_out.at[k],
            dst_ref=part_in.at[k],
            send_sem=part_send.at[k],
            recv_sem=part_recv.at[k],
            device_id=at_z(z + pick(ORDER, k)),
            device_id_type=MESH,
        )

    def step(k, carry):
        for r in (1, 2, 3):

            @pl.when(k == r)
            def _():
                down[r - 1].wait_recv()
                up[r - 1].wait_recv()
                down[r].start()
                up[r].start()
                if r == 1:
                    pltpu.make_async_copy(
                        meta_buf.at[pl.ds(1, NZ - 1)], meta_buf.at[pl.ds(1, NZ - 1)], meta_recv
                    ).wait()

        @pl.when(k == SLOT[4])
        def _():
            down[3].wait_recv()
            up[3].wait_recv()

        @pl.when(k == 0)
        def _():
            x_buf[0] = normed_ref[...]

        @pl.when(k < NZ)
        def _():
            sel = chosen(k, False)
            for c in range(0, width, 512):
                rows_out = jnp.dot(
                    sel, x_buf[k, :, c : c + 512], preferred_element_type=jnp.float32
                )
                snd[k, :, :, c : c + 512] = rows_out.reshape(PLANE, CAP, 512).astype(jnp.bfloat16)
            start_exchange(snd, arr, k, *disp)

        @pl.when((k >= 1) & (k < NZ + 1))
        def _():
            j = k - 1

            @pl.when(j == 0)
            def _():
                for load in loads:
                    load.wait()

            wait_exchange(snd, arr, j, *disp)
            rows_in = arr[j].reshape(PLANE * CAP, width)
            both = jnp.dot(rows_in, w_in[...], preferred_element_type=jnp.float32)
            gate = both[:, :fw]
            inner = (gate * jax.nn.sigmoid(gate) * both[:, fw:]).astype(jnp.bfloat16)
            for c in range(0, width, 512):
                rows_out = jnp.dot(
                    inner, w_down[:, c : c + 512], preferred_element_type=jnp.float32
                )
                res[j, :, :, c : c + 512] = rows_out.reshape(PLANE, CAP, 512).astype(jnp.bfloat16)
            start_exchange(res, ret, j, *back)

        @pl.when(k >= 2)
        def _():
            j = k - 2
            wait_exchange(res, ret, j, *back)
            mix = chosen(j, True)
            for c in range(0, width, 512):
                part = lax.dot_general(
                    mix,
                    ret[j, :, :, c : c + 512].reshape(PLANE * CAP, 512),
                    (((0,), (0,)), ((), ())),
                    preferred_element_type=jnp.float32,
                )

                @pl.when(j == 0)
                def _():
                    acc[:, c : c + 512] = residual_ref[:, c : c + 512] + part

                @pl.when(j > 0)
                def _():
                    part_out[j, :, c : c + 512] = part.astype(jnp.bfloat16)

            @pl.when(j > 0)
            def _():
                part_copy(j).start()

        return carry

    lax.fori_loop(0, NZ + 2, step, 0)

    def gather(k, carry):
        part_copy(k).wait_recv()
        acc[...] += part_in[k].astype(jnp.float32)
        return carry

    lax.fori_loop(1, NZ, gather, 0)
    out_ref[...] = acc[...].astype(jnp.bfloat16)

    for copy in down + up:
        copy.wait_send()
    pltpu.make_async_copy(
        meta_buf.at[pl.ds(1, NZ - 1)], meta_buf.at[pl.ds(1, NZ - 1)], meta_send
    ).wait()

    def drain(k, carry):
        wait_sent(snd, arr, k, *disp)
        wait_sent(res, ret, k, *back)

        @pl.when(k > 0)
        def _():
            part_copy(k).wait_send()

        return carry

    lax.fori_loop(0, NZ, drain, 0)


def moe(normed, residual, meta, expert_gate, expert_up, expert_down):
    rows, width = normed.shape
    fw = expert_gate.shape[2]
    vmem = pl.BlockSpec(memory_space=pltpu.VMEM)
    hbm = pl.BlockSpec(memory_space=pl.ANY)
    dma = pltpu.SemaphoreType.DMA
    slots = pltpu.VMEM((NZ, PLANE, CAP, width), jnp.bfloat16)
    blocks = pltpu.VMEM((NZ, rows, width), jnp.bfloat16)
    return pl.pallas_call(
        moe_kernel,
        out_shape=jax.ShapeDtypeStruct((rows, width), jnp.bfloat16),
        in_specs=[vmem, vmem, vmem, hbm, hbm, hbm],
        out_specs=vmem,
        scratch_shapes=[
            blocks,
            pltpu.VMEM((NZ, 2 * TOP, rows), jnp.float32),
            slots, slots, slots, slots,
            blocks, blocks,
            pltpu.VMEM((rows, width), jnp.float32),
            pltpu.VMEM((width, 2 * fw), jnp.bfloat16),
            pltpu.VMEM((fw, width), jnp.bfloat16),
            dma((NZ + 1,)), dma((NZ + 1,)), dma, dma,
            dma((NZ,)), dma((NZ,)), dma((NZ,)),
            dma((NZ,)), dma((NZ,)), dma((NZ,)),
            dma((NZ,)), dma((NZ,)), dma((3,)),
        ],
        compiler_params=pltpu.CompilerParams(
            collective_id=1, has_side_effects=True, vmem_limit_bytes=VMEM_LIMIT
        ),
        name="moe",
    )(normed, residual, meta, expert_gate, expert_up, expert_down)


def body(
    hidden_in,
    queries,
    keys_values,
    segment_ids,
    routes,
    gate_weights,
    page_table,
    out_weight,
    norm_gain,
    expert_gate,
    expert_up,
    expert_down,
):
    tok_rows = hidden_in.shape[0]
    width = hidden_in.shape[1]
    groups = HQ // HK
    kv_width = HK * HD
    member = lax.axis_index("expert")
    first_row = member * tok_rows
    query_blocks = queries.reshape(tok_rows, HK, groups, HD)
    seg_local = segment_ids.reshape(tok_rows)
    query_pos = first_row + jnp.arange(tok_rows, dtype=jnp.int32)
    last_pos = first_row + tok_rows - 1
    slot_count = tok_rows // PAGE
    table_row = page_table.reshape(-1)
    pages_total = table_row.shape[0]
    targets = member * slot_count + jnp.arange(slot_count, dtype=jnp.int32)
    matches = (table_row[None, :] == targets[:, None]).astype(jnp.int32)
    page_of_slot = jnp.sum(matches * jnp.arange(pages_total, dtype=jnp.int32)[None, :], axis=1)
    score_scale = 1.0 / math.sqrt(HD)

    def attend_block(carried, inputs):
        running_max, running_sum, running_acc = carried
        kv_block, seg_block, block_start = inputs
        row_count = kv_block.shape[0]
        key_part = kv_block[:, :kv_width].reshape(row_count, HK, HD)
        value_part = kv_block[:, kv_width:].reshape(row_count, HK, HD)
        key_pos = block_start + jnp.arange(row_count, dtype=jnp.int32)
        allowed = (key_pos[None, :] <= query_pos[:, None]) & (
            seg_block[None, :] == seg_local[:, None]
        )
        allowed_wide = allowed[:, None, None, :]
        scores = (
            jnp.einsum("thgd,shd->thgs", query_blocks, key_part, preferred_element_type=jnp.float32)
            * score_scale
        )
        masked = jnp.where(allowed_wide, scores, neg_big)
        new_max = jnp.maximum(running_max, jnp.max(masked, axis=3))
        probabilities = jnp.where(allowed_wide, jnp.exp(masked - new_max[..., None]), 0.0)
        factor = jnp.exp(running_max - new_max)
        new_sum = running_sum * factor + jnp.sum(probabilities, axis=3)
        weighted = jnp.einsum(
            "thgs,shd->thgd",
            probabilities.astype(jnp.bfloat16),
            value_part,
            preferred_element_type=jnp.float32,
        )
        new_acc = running_acc * factor[..., None] + weighted
        return (new_max, new_sum, new_acc)

    def keep_state(carried, inputs):
        return carried

    def advance(carried, inputs):
        kv_block, seg_block, block_start = inputs
        row_count = kv_block.shape[0]
        needed = block_start <= last_pos
        return (lax.cond(needed, attend_block, keep_state, carried, inputs), None)

    start_state = (
        jnp.full((tok_rows, HK, groups), neg_big, jnp.float32),
        jnp.zeros((tok_rows, HK, groups), jnp.float32),
        jnp.zeros((tok_rows, HK, groups, HD), jnp.float32),
    )
    start_cache = jnp.zeros((slot_count, PAGE, keys_values.shape[1]), jnp.bfloat16)
    softmax_state = start_state
    cache_slots = start_cache
    kv_piece = lax.all_gather(keys_values, "expert", axis=0, tiled=True)
    seg_piece = lax.all_gather(seg_local, "expert", axis=0, tiled=True)
    piece_rows = kv_piece.shape[0]
    block_rows = math.gcd(piece_rows, 512)
    block_count = piece_rows // block_rows
    kv_steps = kv_piece.reshape(block_count, block_rows, kv_piece.shape[1])
    seg_steps = seg_piece.reshape(block_count, block_rows)
    block_starts = block_rows * jnp.arange(block_count, dtype=jnp.int32)
    softmax_state, _ = lax.scan(advance, softmax_state, (kv_steps, seg_steps, block_starts))
    local_row = page_of_slot * PAGE
    inside = (local_row >= 0) & (local_row < piece_rows)
    safe_row = jnp.clip(local_row, 0, piece_rows - PAGE)

    def take_page(row_start):
        return lax.dynamic_slice_in_dim(kv_piece, row_start, PAGE, 0)

    page_rows = jax.vmap(take_page)(safe_row)
    cache_slots = jnp.where(inside[:, None, None], page_rows, cache_slots)
    final_state, cache_slots = (softmax_state, cache_slots)
    running_max, running_sum, running_acc = final_state
    attended = (
        (running_acc / running_sum[..., None]).reshape(tok_rows, HQ * HD).astype(jnp.bfloat16)
    )
    projected = jnp.dot(
        attended,
        lax.all_gather(out_weight, "dp", axis=0, tiled=True),
        preferred_element_type=jnp.float32,
    )
    residual = hidden_in.astype(jnp.float32) + projected
    normed = (
        residual
        * lax.rsqrt(jnp.mean(residual * residual, axis=1, keepdims=True) + norm_eps)
        * norm_gain
    ).astype(jnp.bfloat16)
    shares = gate_weights / jnp.sum(gate_weights, axis=1, keepdims=True)
    meta = jnp.concatenate([routes.T.astype(jnp.float32), shares.T], axis=0)
    hidden_out = moe(normed, residual, meta, expert_gate, expert_up, expert_down)
    return (hidden_out, cache_slots)


def solution(mesh):
    return jax.shard_map(
        body,
        mesh=mesh,
        in_specs=(
            P(("dp", "expert"), None),
            P(("dp", "expert"), None),
            P(("dp", "expert"), None),
            P("dp", "expert"),
            P(("dp", "expert"), None),
            P(("dp", "expert"), None),
            P("dp", None),
            P("dp", None),
            P(),
            P("expert", None, None),
            P("expert", None, None),
            P("expert", None, None),
        ),
        out_specs=(P(("dp", "expert"), None), P(("dp", "expert"), None, None)),
        check_vma=False,
    )
```

```python
import functools
import math

import jax
import jax.numpy as jnp
from jax import lax
from jax.experimental import pallas as pl
from jax.experimental.pallas import tpu as pltpu
from jax.sharding import PartitionSpec as P

HD = 128
HQ = 16
HK = 2
TOP = 8
PAGE = 16

neg_big = -1e30
norm_eps = 1e-06

NZ, NY, NC = 8, 4, 2
PLANE = NY * NC
CAP = 24
VMEM_LIMIT = 64 * 1024 * 1024 - 2 * 1024 * 1024
MESH = pl.DeviceIdType.MESH
ORDER = (0, 1, 2, -2, 3, -3, 4, -1)
SLOT = {d: k for k, d in enumerate(ORDER)}


def pick(table, k):
    if isinstance(k, int):
        return table[k]
    value = jnp.int32(table[0])
    for j in range(1, len(table)):
        value = jnp.where(k == j, jnp.int32(table[j]), value)
    return value


def moe_kernel(
    normed_ref, residual_ref, meta_ref, wg_hbm, wu_hbm, wd_hbm, out_ref,
    x_buf, meta_buf, snd, arr, res, ret, part_out, part_in, acc, w_in, w_down,
    ring_send, ring_recv, meta_send, meta_recv, disp_send, disp_recv, disp_self,
    back_send, back_recv, back_self, part_send, part_recv, weight_sem,
):
    me = lax.axis_index("expert")
    z = me // PLANE
    pos = me % PLANE
    rows, width = normed_ref.shape
    fw = w_down.shape[0]

    def at_z(target):
        return {"expert": lax.rem(target + 2 * NZ, NZ) * PLANE + pos}

    def at_plane(target):
        return {"expert": z * PLANE + target}

    loads = [
        pltpu.make_async_copy(wg_hbm.at[0], w_in.at[:, pl.ds(0, fw)], weight_sem.at[0]),
        pltpu.make_async_copy(wu_hbm.at[0], w_in.at[:, pl.ds(fw, fw)], weight_sem.at[1]),
        pltpu.make_async_copy(wd_hbm.at[0], w_down, weight_sem.at[2]),
    ]
    for load in loads:
        load.start()

    barrier = pltpu.get_barrier_semaphore()
    for d in range(1, NZ):
        pl.semaphore_signal(barrier, inc=1, device_id=at_z(z + d), device_id_type=MESH)
    for o in range(1, PLANE):
        pl.semaphore_signal(
            barrier, inc=1, device_id=at_plane(lax.rem(pos + o, PLANE)), device_id_type=MESH
        )
    pl.semaphore_wait(barrier, NZ - 1 + PLANE - 1)

    def ring_copy(src, slot, sem, toward, first=0, count=None):
        count = rows if count is None else count
        return pltpu.make_async_remote_copy(
            src_ref=src.at[pl.ds(first, count)],
            dst_ref=x_buf.at[slot, pl.ds(first, count)],
            send_sem=ring_send.at[sem],
            recv_sem=ring_recv.at[sem],
            device_id=at_z(z + toward),
            device_id_type=MESH,
        )

    half = rows // 2
    down = [ring_copy(normed_ref, SLOT[1], SLOT[1], -1)]
    up = [ring_copy(normed_ref, SLOT[-1], SLOT[-1], 1)]
    for d in (1, 2):
        down.append(ring_copy(x_buf.at[SLOT[d]], SLOT[d + 1], SLOT[d + 1], -1))
        up.append(ring_copy(x_buf.at[SLOT[-d]], SLOT[-d - 1], SLOT[-d - 1], 1))
    down.append(ring_copy(x_buf.at[SLOT[3]], SLOT[4], SLOT[4], -1, 0, half))
    up.append(ring_copy(x_buf.at[SLOT[-3]], SLOT[4], NZ, 1, half, half))

    down[0].start()
    up[0].start()
    for k in range(1, NZ):
        copy = pltpu.make_async_remote_copy(
            src_ref=meta_ref,
            dst_ref=meta_buf.at[k],
            send_sem=meta_send,
            recv_sem=meta_recv,
            device_id=at_z(z - ORDER[k]),
            device_id_type=MESH,
        )
        copy.start()
    meta_buf[0] = meta_ref[...]

    row_id = lax.broadcasted_iota(jnp.int32, (rows, rows), 0)
    col_id = lax.broadcasted_iota(jnp.int32, (rows, rows), 1)
    earlier = (row_id < col_id).astype(jnp.bfloat16)
    first_expert = z * PLANE
    expert_id = (first_expert + lax.broadcasted_iota(jnp.int32, (PLANE, rows), 0)).astype(
        jnp.float32
    )
    slot_id = lax.broadcasted_iota(jnp.int32, (CAP, rows), 0).astype(jnp.float32)

    def chosen(k, weighted):
        meta = meta_buf[k]
        mask = jnp.zeros((PLANE, rows), jnp.float32)
        share = jnp.zeros((PLANE, rows), jnp.float32)
        for n in range(TOP):
            hit = meta[n : n + 1, :] == expert_id
            mask = jnp.where(hit, 1.0, mask)
            if weighted:
                share = jnp.where(hit, meta[TOP + n : TOP + n + 1, :], share)
        rank = jnp.dot(mask.astype(jnp.bfloat16), earlier, preferred_element_type=jnp.float32)
        rank = jnp.where(mask > 0.5, rank, -1.0)
        value = share if weighted else mask
        pieces = [
            jnp.where(rank[e : e + 1, :] == slot_id, value[e : e + 1, :], 0.0)
            for e in range(PLANE)
        ]
        return jnp.concatenate(pieces, axis=0).astype(jnp.bfloat16)

    def exchange(src, dst, k, send_sem, recv_sem, self_sem):
        copies = []
        for o in range(1, PLANE):
            target = lax.rem(pos + o, PLANE)
            copies.append(
                pltpu.make_async_remote_copy(
                    src_ref=src.at[k, target],
                    dst_ref=dst.at[k, pos],
                    send_sem=send_sem.at[k],
                    recv_sem=recv_sem.at[k],
                    device_id=at_plane(target),
                    device_id_type=MESH,
                )
            )
        own = pltpu.make_async_copy(src.at[k, pos], dst.at[k, pos], self_sem.at[k])
        return copies, own

    def start_exchange(*args):
        copies, own = exchange(*args)
        for copy in copies:
            copy.start()
        own.start()

    def others(buf, k):
        return buf.at[k, pl.ds(0, PLANE - 1)]

    def wait_exchange(src, dst, k, send_sem, recv_sem, self_sem):
        pltpu.make_async_copy(others(dst, k), others(dst, k), recv_sem.at[k]).wait()
        pltpu.make_async_copy(src.at[k, pos], dst.at[k, pos], self_sem.at[k]).wait()

    def wait_sent(src, dst, k, send_sem, recv_sem, self_sem):
        pltpu.make_async_copy(others(src, k), others(src, k), send_sem.at[k]).wait()

    disp = (disp_send, disp_recv, disp_self)
    back = (back_send, back_recv, back_self)

    def part_copy(k):
        return pltpu.make_async_remote_copy(
            src_ref=part_out.at[k],
            dst_ref=part_in.at[k],
            send_sem=part_send.at[k],
            recv_sem=part_recv.at[k],
            device_id=at_z(z + pick(ORDER, k)),
            device_id_type=MESH,
        )

    def step(k, carry):
        for r in (1, 2, 3):

            @pl.when(k == r)
            def _():
                down[r - 1].wait_recv()
                up[r - 1].wait_recv()
                down[r].start()
                up[r].start()
                if r == 1:
                    pltpu.make_async_copy(
                        meta_buf.at[pl.ds(1, NZ - 1)], meta_buf.at[pl.ds(1, NZ - 1)], meta_recv
                    ).wait()

        @pl.when(k == SLOT[4])
        def _():
            down[3].wait_recv()
            up[3].wait_recv()

        @pl.when(k == 0)
        def _():
            x_buf[0] = normed_ref[...]

        @pl.when(k < NZ)
        def _():
            sel = chosen(k, False)
            for c in range(0, width, 512):
                rows_out = jnp.dot(
                    sel, x_buf[k, :, c : c + 512], preferred_element_type=jnp.float32
                )
                snd[k, :, :, c : c + 512] = rows_out.reshape(PLANE, CAP, 512).astype(jnp.bfloat16)
            start_exchange(snd, arr, k, *disp)

        @pl.when((k >= 1) & (k < NZ + 1))
        def _():
            j = k - 1

            @pl.when(j == 0)
            def _():
                for load in loads:
                    load.wait()

            wait_exchange(snd, arr, j, *disp)
            rows_in = arr[j].reshape(PLANE * CAP, width)
            both = jnp.dot(rows_in, w_in[...], preferred_element_type=jnp.float32)
            gate = both[:, :fw]
            inner = (gate * jax.nn.sigmoid(gate) * both[:, fw:]).astype(jnp.bfloat16)
            for c in range(0, width, 512):
                rows_out = jnp.dot(
                    inner, w_down[:, c : c + 512], preferred_element_type=jnp.float32
                )
                res[j, :, :, c : c + 512] = rows_out.reshape(PLANE, CAP, 512).astype(jnp.bfloat16)
            start_exchange(res, ret, j, *back)

        @pl.when(k >= 2)
        def _():
            j = k - 2
            wait_exchange(res, ret, j, *back)
            mix = chosen(j, True)
            for c in range(0, width, 512):
                part = lax.dot_general(
                    mix,
                    ret[j, :, :, c : c + 512].reshape(PLANE * CAP, 512),
                    (((0,), (0,)), ((), ())),
                    preferred_element_type=jnp.float32,
                )

                @pl.when(j == 0)
                def _():
                    acc[:, c : c + 512] = residual_ref[:, c : c + 512] + part

                @pl.when(j > 0)
                def _():
                    part_out[j, :, c : c + 512] = part.astype(jnp.bfloat16)

            @pl.when(j > 0)
            def _():
                part_copy(j).start()

        return carry

    lax.fori_loop(0, NZ + 2, step, 0)

    def gather(k, carry):
        part_copy(k).wait_recv()
        acc[...] += part_in[k].astype(jnp.float32)
        return carry

    lax.fori_loop(1, NZ, gather, 0)
    out_ref[...] = acc[...].astype(jnp.bfloat16)

    for copy in down + up:
        copy.wait_send()
    pltpu.make_async_copy(
        meta_buf.at[pl.ds(1, NZ - 1)], meta_buf.at[pl.ds(1, NZ - 1)], meta_send
    ).wait()

    def drain(k, carry):
        wait_sent(snd, arr, k, *disp)
        wait_sent(res, ret, k, *back)

        @pl.when(k > 0)
        def _():
            part_copy(k).wait_send()

        return carry

    lax.fori_loop(0, NZ, drain, 0)


def moe(normed, residual, meta, expert_gate, expert_up, expert_down):
    rows, width = normed.shape
    fw = expert_gate.shape[2]
    vmem = pl.BlockSpec(memory_space=pltpu.VMEM)
    hbm = pl.BlockSpec(memory_space=pl.ANY)
    dma = pltpu.SemaphoreType.DMA
    slots = pltpu.VMEM((NZ, PLANE, CAP, width), jnp.bfloat16)
    blocks = pltpu.VMEM((NZ, rows, width), jnp.bfloat16)
    return pl.pallas_call(
        moe_kernel,
        out_shape=jax.ShapeDtypeStruct((rows, width), jnp.bfloat16),
        in_specs=[vmem, vmem, vmem, hbm, hbm, hbm],
        out_specs=vmem,
        scratch_shapes=[
            blocks,
            pltpu.VMEM((NZ, 2 * TOP, rows), jnp.float32),
            slots, slots, slots, slots,
            blocks, blocks,
            pltpu.VMEM((rows, width), jnp.float32),
            pltpu.VMEM((width, 2 * fw), jnp.bfloat16),
            pltpu.VMEM((fw, width), jnp.bfloat16),
            dma((NZ + 1,)), dma((NZ + 1,)), dma, dma,
            dma((NZ,)), dma((NZ,)), dma((NZ,)),
            dma((NZ,)), dma((NZ,)), dma((NZ,)),
            dma((NZ,)), dma((NZ,)), dma((3,)),
        ],
        compiler_params=pltpu.CompilerParams(
            collective_id=1, has_side_effects=True, vmem_limit_bytes=VMEM_LIMIT
        ),
        name="moe",
    )(normed, residual, meta, expert_gate, expert_up, expert_down)


def spread_kernel(
    seg_ref, weight_ref, seg_out, weight_out,
    seg_buf, seg_send, seg_recv, own_sem, x_send, x_recv, core_send, core_recv,
):
    members = seg_out.shape[0]
    me = lax.axis_index("expert")
    col = lax.axis_index("dp")
    n_dp = lax.axis_size("dp")
    block = weight_ref.shape[0]
    half = block // NC
    core = lax.rem(me, NC)

    def peer(o):
        return {"expert": lax.rem(me + o, members)}

    def at_dp(o):
        return {"dp": lax.rem(col + o, n_dp)}

    barrier = pltpu.get_barrier_semaphore()
    for o in range(1, n_dp):
        pl.semaphore_signal(barrier, inc=1, device_id=at_dp(o), device_id_type=MESH)

    def greet(o, carry):
        pl.semaphore_signal(barrier, inc=1, device_id=peer(o), device_id_type=MESH)
        return carry

    lax.fori_loop(1, members, greet, 0)
    pl.semaphore_wait(barrier, members - 1 + n_dp - 1)

    mine = pl.ds(pl.multiple_of(core * half, half), half)
    hops = (1, 3, 2)

    def rows_of(source):
        return pl.ds(pl.multiple_of(source * block + core * half, half), half)

    across = {}
    for o in hops:
        across[o] = pltpu.make_async_remote_copy(
            src_ref=weight_ref.at[mine],
            dst_ref=weight_out.at[rows_of(col)],
            send_sem=x_send.at[o],
            recv_sem=x_recv.at[o],
            device_id=at_dp(o),
            device_id_type=MESH,
        )
        across[o].start()

    def send_seg(o, carry):
        pltpu.make_async_remote_copy(
            src_ref=seg_ref,
            dst_ref=seg_buf.at[me],
            send_sem=seg_send,
            recv_sem=seg_recv,
            device_id=peer(o),
            device_id_type=MESH,
        ).start()
        return carry

    lax.fori_loop(1, members, send_seg, 0)
    own = pltpu.make_async_copy(
        weight_ref, weight_out.at[pl.ds(pl.multiple_of(col * block, block), block)], own_sem
    )
    own.start()
    seg_buf[me] = seg_ref[...]

    over = {}
    for o in hops:
        across[o].wait_recv()
        came = rows_of(lax.rem(col - o + n_dp, n_dp))
        over[o] = pltpu.make_async_remote_copy(
            src_ref=weight_out.at[came],
            dst_ref=weight_out.at[came],
            send_sem=core_send.at[o],
            recv_sem=core_recv.at[o],
            device_id={"expert": me + 1 - 2 * core},
            device_id_type=MESH,
        )
        over[o].start()

    others = seg_buf.at[pl.ds(0, members - 1)]
    pltpu.make_async_copy(others, others, seg_recv).wait()
    seg_out[...] = seg_buf[...]
    pltpu.make_async_copy(others, others, seg_send).wait()
    own.wait()
    for o in hops:
        across[o].wait_send()
        over[o].wait_send()
        over[o].wait_recv()


def spread(seg_rows, out_weight):
    members = lax.axis_size("expert")
    n_dp = lax.axis_size("dp")
    block, width = out_weight.shape
    vmem = pl.BlockSpec(memory_space=pltpu.VMEM)
    hbm = pl.BlockSpec(memory_space=pl.ANY)
    dma = pltpu.SemaphoreType.DMA
    seg_shape = (members,) + seg_rows.shape
    return pl.pallas_call(
        spread_kernel,
        out_shape=(
            jax.ShapeDtypeStruct(seg_shape, jnp.int32),
            jax.ShapeDtypeStruct((n_dp * block, width), out_weight.dtype),
        ),
        in_specs=[vmem, vmem],
        out_specs=(vmem, hbm),
        scratch_shapes=[
            pltpu.VMEM(seg_shape, jnp.int32),
            dma, dma, dma,
            dma((n_dp,)), dma((n_dp,)), dma((n_dp,)), dma((n_dp,)),
        ],
        compiler_params=pltpu.CompilerParams(collective_id=2, has_side_effects=True),
        cost_estimate=pl.CostEstimate(flops=0, bytes_accessed=150_000_000, transcendentals=0),
        name="spread",
    )(seg_rows, out_weight)


def pages_kernel(page_ref, rows_hbm, out_ref, sems):
    count = out_ref.shape[0]
    last = rows_hbm.shape[0] // PAGE - 1
    copies = []
    for n in range(count):
        page = jnp.minimum(jnp.maximum(page_ref[n], 0), last)
        copies.append(
            pltpu.make_async_copy(
                rows_hbm.at[pl.ds(pl.multiple_of(page * PAGE, PAGE), PAGE)],
                out_ref.at[n],
                sems.at[n],
            )
        )
        copies[-1].start()
    for copy in copies:
        copy.wait()


def take_pages(pages, rows):
    count = pages.shape[0]
    return pl.pallas_call(
        pages_kernel,
        out_shape=jax.ShapeDtypeStruct((count, PAGE, rows.shape[1]), rows.dtype),
        in_specs=[
            pl.BlockSpec(memory_space=pltpu.SMEM),
            pl.BlockSpec(memory_space=pl.ANY),
        ],
        out_specs=pl.BlockSpec(memory_space=pltpu.VMEM),
        scratch_shapes=[pltpu.SemaphoreType.DMA((count,))],
        name="pages",
    )(pages, rows)


def body(
    hidden_in,
    queries,
    keys_values,
    segment_ids,
    routes,
    gate_weights,
    page_table,
    out_weight,
    norm_gain,
    expert_gate,
    expert_up,
    expert_down,
):
    tok_rows = hidden_in.shape[0]
    width = hidden_in.shape[1]
    groups = HQ // HK
    kv_width = HK * HD
    member = lax.axis_index("expert")
    first_row = member * tok_rows
    query_blocks = queries.reshape(tok_rows, HK, groups, HD)
    seg_local = segment_ids.reshape(tok_rows)
    query_pos = first_row + jnp.arange(tok_rows, dtype=jnp.int32)
    last_pos = first_row + tok_rows - 1
    slot_count = tok_rows // PAGE
    table_row = page_table.reshape(-1)
    pages_total = table_row.shape[0]
    targets = member * slot_count + jnp.arange(slot_count, dtype=jnp.int32)
    matches = (table_row[None, :] == targets[:, None]).astype(jnp.int32)
    page_of_slot = jnp.sum(matches * jnp.arange(pages_total, dtype=jnp.int32)[None, :], axis=1)
    score_scale = 1.0 / math.sqrt(HD)

    def attend_block(carried, inputs):
        running_max, running_sum, running_acc = carried
        kv_block, seg_block, block_start = inputs
        row_count = kv_block.shape[0]
        key_part = kv_block[:, :kv_width].reshape(row_count, HK, HD)
        value_part = kv_block[:, kv_width:].reshape(row_count, HK, HD)
        key_pos = block_start + jnp.arange(row_count, dtype=jnp.int32)
        allowed = (key_pos[None, :] <= query_pos[:, None]) & (
            seg_block[None, :] == seg_local[:, None]
        )
        allowed_wide = allowed[:, None, None, :]
        scores = (
            jnp.einsum("thgd,shd->thgs", query_blocks, key_part, preferred_element_type=jnp.float32)
            * score_scale
        )
        masked = jnp.where(allowed_wide, scores, neg_big)
        new_max = jnp.maximum(running_max, jnp.max(masked, axis=3))
        probabilities = jnp.where(allowed_wide, jnp.exp(masked - new_max[..., None]), 0.0)
        factor = jnp.exp(running_max - new_max)
        new_sum = running_sum * factor + jnp.sum(probabilities, axis=3)
        weighted = jnp.einsum(
            "thgs,shd->thgd",
            probabilities.astype(jnp.bfloat16),
            value_part,
            preferred_element_type=jnp.float32,
        )
        new_acc = running_acc * factor[..., None] + weighted
        return (new_max, new_sum, new_acc)

    def keep_state(carried, inputs):
        return carried

    def advance(carried, inputs):
        kv_block, seg_block, block_start = inputs
        row_count = kv_block.shape[0]
        needed = block_start <= last_pos
        return (lax.cond(needed, attend_block, keep_state, carried, inputs), None)

    start_state = (
        jnp.full((tok_rows, HK, groups), neg_big, jnp.float32),
        jnp.zeros((tok_rows, HK, groups), jnp.float32),
        jnp.zeros((tok_rows, HK, groups, HD), jnp.float32),
    )
    softmax_state = start_state
    kv_piece = lax.all_gather(keys_values, "expert", axis=0, tiled=True)
    seg_all, weight_all = spread(jnp.broadcast_to(seg_local[None, :], (8, tok_rows)), out_weight)
    seg_piece = seg_all[:, 0, :].reshape(-1)
    piece_rows = kv_piece.shape[0]
    block_rows = math.gcd(piece_rows, 512)
    block_count = piece_rows // block_rows
    kv_steps = kv_piece.reshape(block_count, block_rows, kv_piece.shape[1])
    seg_steps = seg_piece.reshape(block_count, block_rows)
    block_starts = block_rows * jnp.arange(block_count, dtype=jnp.int32)
    softmax_state, _ = lax.scan(advance, softmax_state, (kv_steps, seg_steps, block_starts))
    cache_slots = take_pages(page_of_slot, kv_piece)
    running_max, running_sum, running_acc = softmax_state
    attended = (
        (running_acc / running_sum[..., None]).reshape(tok_rows, HQ * HD).astype(jnp.bfloat16)
    )
    projected = jnp.dot(
        attended,
        weight_all,
        preferred_element_type=jnp.float32,
    )
    residual = hidden_in.astype(jnp.float32) + projected
    normed = (
        residual
        * lax.rsqrt(jnp.mean(residual * residual, axis=1, keepdims=True) + norm_eps)
        * norm_gain
    ).astype(jnp.bfloat16)
    shares = gate_weights / jnp.sum(gate_weights, axis=1, keepdims=True)
    meta = jnp.concatenate([routes.T.astype(jnp.float32), shares.T], axis=0)
    hidden_out = moe(normed, residual, meta, expert_gate, expert_up, expert_down)
    return (hidden_out, cache_slots)


def solution(mesh):
    return jax.shard_map(
        body,
        mesh=mesh,
        in_specs=(
            P(("dp", "expert"), None),
            P(("dp", "expert"), None),
            P(("dp", "expert"), None),
            P("dp", "expert"),
            P(("dp", "expert"), None),
            P(("dp", "expert"), None),
            P("dp", None),
            P("dp", None),
            P(),
            P("expert", None, None),
            P("expert", None, None),
            P("expert", None, None),
        ),
        out_specs=(P(("dp", "expert"), None), P(("dp", "expert"), None, None)),
        check_vma=False,
    )
```

```python
import functools
import math

import jax
import jax.numpy as jnp
from jax import lax
from jax.experimental import pallas as pl
from jax.experimental.pallas import tpu as pltpu
from jax.sharding import PartitionSpec as P

HD = 128
HQ = 16
HK = 2
TOP = 8
PAGE = 16

neg_big = -1e30
norm_eps = 1e-06

NZ, NY, NC = 8, 4, 2
PLANE = NY * NC
CAP = 24
LAG = 2
VMEM_LIMIT = 64 * 1024 * 1024 - 2 * 1024 * 1024
MESH = pl.DeviceIdType.MESH
ORDER = (0, 1, 2, -2, 3, -3, 4, -1)
SLOT = {d: k for k, d in enumerate(ORDER)}


def pick(table, k):
    if isinstance(k, int):
        return table[k]
    value = jnp.int32(table[0])
    for j in range(1, len(table)):
        value = jnp.where(k == j, jnp.int32(table[j]), value)
    return value


def moe_kernel(
    normed_ref, residual_ref, meta_ref, wg_hbm, wu_hbm, wd_hbm, out_ref,
    x_buf, meta_buf, snd, arr, res, ret, part_out, part_in, acc, w_in, w_down,
    ring_send, ring_recv, meta_send, meta_recv, disp_send, disp_recv, disp_self,
    back_send, back_recv, back_self, part_send, part_recv, weight_sem,
):
    me = lax.axis_index("expert")
    z = me // PLANE
    pos = me % PLANE
    rows, width = normed_ref.shape
    fw = w_down.shape[0]

    def at_z(target):
        return {"expert": lax.rem(target + 2 * NZ, NZ) * PLANE + pos}

    def at_plane(target):
        return {"expert": z * PLANE + target}

    loads = [
        pltpu.make_async_copy(wg_hbm.at[0], w_in.at[:, pl.ds(0, fw)], weight_sem.at[0]),
        pltpu.make_async_copy(wu_hbm.at[0], w_in.at[:, pl.ds(fw, fw)], weight_sem.at[1]),
        pltpu.make_async_copy(wd_hbm.at[0], w_down, weight_sem.at[2]),
    ]
    for load in loads:
        load.start()

    barrier = pltpu.get_barrier_semaphore()
    for d in range(1, NZ):
        pl.semaphore_signal(barrier, inc=1, device_id=at_z(z + d), device_id_type=MESH)
    for o in range(1, PLANE):
        pl.semaphore_signal(
            barrier, inc=1, device_id=at_plane(lax.rem(pos + o, PLANE)), device_id_type=MESH
        )
    pl.semaphore_wait(barrier, NZ - 1 + PLANE - 1)

    def ring_copy(src, slot, sem, toward, first=0, count=None):
        count = rows if count is None else count
        return pltpu.make_async_remote_copy(
            src_ref=src.at[pl.ds(first, count)],
            dst_ref=x_buf.at[slot, pl.ds(first, count)],
            send_sem=ring_send.at[sem],
            recv_sem=ring_recv.at[sem],
            device_id=at_z(z + toward),
            device_id_type=MESH,
        )

    half = rows // 2
    down = [ring_copy(normed_ref, SLOT[1], SLOT[1], -1)]
    up = [ring_copy(normed_ref, SLOT[-1], SLOT[-1], 1)]
    for d in (1, 2):
        down.append(ring_copy(x_buf.at[SLOT[d]], SLOT[d + 1], SLOT[d + 1], -1))
        up.append(ring_copy(x_buf.at[SLOT[-d]], SLOT[-d - 1], SLOT[-d - 1], 1))
    down.append(ring_copy(x_buf.at[SLOT[3]], SLOT[4], SLOT[4], -1, 0, half))
    up.append(ring_copy(x_buf.at[SLOT[-3]], SLOT[4], NZ, 1, half, half))

    down[0].start()
    up[0].start()
    for k in range(1, NZ):
        copy = pltpu.make_async_remote_copy(
            src_ref=meta_ref,
            dst_ref=meta_buf.at[k],
            send_sem=meta_send,
            recv_sem=meta_recv,
            device_id=at_z(z - ORDER[k]),
            device_id_type=MESH,
        )
        copy.start()
    meta_buf[0] = meta_ref[...]

    row_id = lax.broadcasted_iota(jnp.int32, (rows, rows), 0)
    col_id = lax.broadcasted_iota(jnp.int32, (rows, rows), 1)
    earlier = (row_id < col_id).astype(jnp.bfloat16)
    first_expert = z * PLANE
    expert_id = (first_expert + lax.broadcasted_iota(jnp.int32, (PLANE, rows), 0)).astype(
        jnp.float32
    )
    slot_id = lax.broadcasted_iota(jnp.int32, (CAP, rows), 0).astype(jnp.float32)

    def chosen(k, weighted):
        meta = meta_buf[k]
        mask = jnp.zeros((PLANE, rows), jnp.float32)
        share = jnp.zeros((PLANE, rows), jnp.float32)
        for n in range(TOP):
            hit = meta[n : n + 1, :] == expert_id
            mask = jnp.where(hit, 1.0, mask)
            if weighted:
                share = jnp.where(hit, meta[TOP + n : TOP + n + 1, :], share)
        rank = jnp.dot(mask.astype(jnp.bfloat16), earlier, preferred_element_type=jnp.float32)
        rank = jnp.where(mask > 0.5, rank, -1.0)
        value = share if weighted else mask
        pieces = [
            jnp.where(rank[e : e + 1, :] == slot_id, value[e : e + 1, :], 0.0)
            for e in range(PLANE)
        ]
        return jnp.concatenate(pieces, axis=0).astype(jnp.bfloat16)

    def exchange(src, dst, k, send_sem, recv_sem, self_sem):
        copies = []
        for o in range(1, PLANE):
            target = lax.rem(pos + o, PLANE)
            copies.append(
                pltpu.make_async_remote_copy(
                    src_ref=src.at[k, target],
                    dst_ref=dst.at[k, pos],
                    send_sem=send_sem.at[k],
                    recv_sem=recv_sem.at[k],
                    device_id=at_plane(target),
                    device_id_type=MESH,
                )
            )
        own = pltpu.make_async_copy(src.at[k, pos], dst.at[k, pos], self_sem.at[k])
        return copies, own

    def start_exchange(*args):
        copies, own = exchange(*args)
        for copy in copies:
            copy.start()
        own.start()

    def others(buf, k):
        return buf.at[k, pl.ds(0, PLANE - 1)]

    def wait_exchange(src, dst, k, send_sem, recv_sem, self_sem):
        pltpu.make_async_copy(others(dst, k), others(dst, k), recv_sem.at[k]).wait()
        pltpu.make_async_copy(src.at[k, pos], dst.at[k, pos], self_sem.at[k]).wait()

    def wait_sent(src, dst, k, send_sem, recv_sem, self_sem):
        pltpu.make_async_copy(others(src, k), others(src, k), send_sem.at[k]).wait()

    disp = (disp_send, disp_recv, disp_self)
    back = (back_send, back_recv, back_self)

    def part_copy(k):
        return pltpu.make_async_remote_copy(
            src_ref=part_out.at[k],
            dst_ref=part_in.at[k],
            send_sem=part_send.at[k],
            recv_sem=part_recv.at[k],
            device_id=at_z(z + pick(ORDER, k)),
            device_id_type=MESH,
        )

    def step(k, carry):
        for r in (1, 2, 3):

            @pl.when(k == r)
            def _():
                down[r - 1].wait_recv()
                up[r - 1].wait_recv()
                down[r].start()
                up[r].start()
                if r == 1:
                    pltpu.make_async_copy(
                        meta_buf.at[pl.ds(1, NZ - 1)], meta_buf.at[pl.ds(1, NZ - 1)], meta_recv
                    ).wait()

        @pl.when(k == SLOT[4])
        def _():
            down[3].wait_recv()
            up[3].wait_recv()

        @pl.when(k == 0)
        def _():
            x_buf[0] = normed_ref[...]

        @pl.when(k < NZ)
        def _():
            sel = chosen(k, False)
            for c in range(0, width, 512):
                rows_out = jnp.dot(
                    sel, x_buf[k, :, c : c + 512], preferred_element_type=jnp.float32
                )
                snd[k, :, :, c : c + 512] = rows_out.reshape(PLANE, CAP, 512).astype(jnp.bfloat16)
            start_exchange(snd, arr, k, *disp)

        @pl.when((k >= LAG) & (k < NZ + LAG))
        def _():
            j = k - LAG

            @pl.when(j == 0)
            def _():
                for load in loads:
                    load.wait()

            wait_exchange(snd, arr, j, *disp)
            rows_in = arr[j].reshape(PLANE * CAP, width)
            both = jnp.dot(rows_in, w_in[...], preferred_element_type=jnp.float32)
            gate = both[:, :fw]
            inner = (gate * jax.nn.sigmoid(gate) * both[:, fw:]).astype(jnp.bfloat16)
            for c in range(0, width, 512):
                rows_out = jnp.dot(
                    inner, w_down[:, c : c + 512], preferred_element_type=jnp.float32
                )
                res[j, :, :, c : c + 512] = rows_out.reshape(PLANE, CAP, 512).astype(jnp.bfloat16)
            start_exchange(res, ret, j, *back)

        @pl.when(k >= 2 * LAG)
        def _():
            j = k - 2 * LAG
            wait_exchange(res, ret, j, *back)
            mix = chosen(j, True)
            for c in range(0, width, 512):
                part = lax.dot_general(
                    mix,
                    ret[j, :, :, c : c + 512].reshape(PLANE * CAP, 512),
                    (((0,), (0,)), ((), ())),
                    preferred_element_type=jnp.float32,
                )

                @pl.when(j == 0)
                def _():
                    acc[:, c : c + 512] = residual_ref[:, c : c + 512] + part

                @pl.when(j > 0)
                def _():
                    part_out[j, :, c : c + 512] = part.astype(jnp.bfloat16)

            @pl.when(j > 0)
            def _():
                part_copy(j).start()

        return carry

    lax.fori_loop(0, NZ + 2 * LAG, step, 0)

    def gather(k, carry):
        part_copy(k).wait_recv()
        acc[...] += part_in[k].astype(jnp.float32)
        return carry

    lax.fori_loop(1, NZ, gather, 0)
    out_ref[...] = acc[...].astype(jnp.bfloat16)

    for copy in down + up:
        copy.wait_send()
    pltpu.make_async_copy(
        meta_buf.at[pl.ds(1, NZ - 1)], meta_buf.at[pl.ds(1, NZ - 1)], meta_send
    ).wait()

    def drain(k, carry):
        wait_sent(snd, arr, k, *disp)
        wait_sent(res, ret, k, *back)

        @pl.when(k > 0)
        def _():
            part_copy(k).wait_send()

        return carry

    lax.fori_loop(0, NZ, drain, 0)


def moe(normed, residual, meta, expert_gate, expert_up, expert_down):
    rows, width = normed.shape
    fw = expert_gate.shape[2]
    vmem = pl.BlockSpec(memory_space=pltpu.VMEM)
    hbm = pl.BlockSpec(memory_space=pl.ANY)
    dma = pltpu.SemaphoreType.DMA
    slots = pltpu.VMEM((NZ, PLANE, CAP, width), jnp.bfloat16)
    blocks = pltpu.VMEM((NZ, rows, width), jnp.bfloat16)
    return pl.pallas_call(
        moe_kernel,
        out_shape=jax.ShapeDtypeStruct((rows, width), jnp.bfloat16),
        in_specs=[vmem, vmem, vmem, hbm, hbm, hbm],
        out_specs=vmem,
        scratch_shapes=[
            blocks,
            pltpu.VMEM((NZ, 2 * TOP, rows), jnp.float32),
            slots, slots, slots, slots,
            blocks, blocks,
            pltpu.VMEM((rows, width), jnp.float32),
            pltpu.VMEM((width, 2 * fw), jnp.bfloat16),
            pltpu.VMEM((fw, width), jnp.bfloat16),
            dma((NZ + 1,)), dma((NZ + 1,)), dma, dma,
            dma((NZ,)), dma((NZ,)), dma((NZ,)),
            dma((NZ,)), dma((NZ,)), dma((NZ,)),
            dma((NZ,)), dma((NZ,)), dma((3,)),
        ],
        compiler_params=pltpu.CompilerParams(
            collective_id=1, has_side_effects=True, vmem_limit_bytes=VMEM_LIMIT
        ),
        name="moe",
    )(normed, residual, meta, expert_gate, expert_up, expert_down)


def spread_kernel(
    seg_ref, weight_ref, seg_out, weight_out,
    seg_buf, seg_send, seg_recv, own_sem, x_send, x_recv, core_send, core_recv,
):
    members = seg_out.shape[0]
    me = lax.axis_index("expert")
    col = lax.axis_index("dp")
    n_dp = lax.axis_size("dp")
    block = weight_ref.shape[0]
    half = block // NC
    core = lax.rem(me, NC)

    def peer(o):
        return {"expert": lax.rem(me + o, members)}

    def at_dp(o):
        return {"dp": lax.rem(col + o, n_dp)}

    barrier = pltpu.get_barrier_semaphore()
    for o in range(1, n_dp):
        pl.semaphore_signal(barrier, inc=1, device_id=at_dp(o), device_id_type=MESH)

    def greet(o, carry):
        pl.semaphore_signal(barrier, inc=1, device_id=peer(o), device_id_type=MESH)
        return carry

    lax.fori_loop(1, members, greet, 0)
    pl.semaphore_wait(barrier, members - 1 + n_dp - 1)

    mine = pl.ds(pl.multiple_of(core * half, half), half)
    hops = (1, 3, 2)

    def rows_of(source):
        return pl.ds(pl.multiple_of(source * block + core * half, half), half)

    across = {}
    for o in hops:
        across[o] = pltpu.make_async_remote_copy(
            src_ref=weight_ref.at[mine],
            dst_ref=weight_out.at[rows_of(col)],
            send_sem=x_send.at[o],
            recv_sem=x_recv.at[o],
            device_id=at_dp(o),
            device_id_type=MESH,
        )
        across[o].start()

    def send_seg(o, carry):
        pltpu.make_async_remote_copy(
            src_ref=seg_ref,
            dst_ref=seg_buf.at[me],
            send_sem=seg_send,
            recv_sem=seg_recv,
            device_id=peer(o),
            device_id_type=MESH,
        ).start()
        return carry

    lax.fori_loop(1, members, send_seg, 0)
    own = pltpu.make_async_copy(
        weight_ref, weight_out.at[pl.ds(pl.multiple_of(col * block, block), block)], own_sem
    )
    own.start()
    seg_buf[me] = seg_ref[...]

    over = {}
    for o in hops:
        across[o].wait_recv()
        came = rows_of(lax.rem(col - o + n_dp, n_dp))
        over[o] = pltpu.make_async_remote_copy(
            src_ref=weight_out.at[came],
            dst_ref=weight_out.at[came],
            send_sem=core_send.at[o],
            recv_sem=core_recv.at[o],
            device_id={"expert": me + 1 - 2 * core},
            device_id_type=MESH,
        )
        over[o].start()

    others = seg_buf.at[pl.ds(0, members - 1)]
    pltpu.make_async_copy(others, others, seg_recv).wait()
    seg_out[...] = seg_buf[...]
    pltpu.make_async_copy(others, others, seg_send).wait()
    own.wait()
    for o in hops:
        across[o].wait_send()
        over[o].wait_send()
        over[o].wait_recv()


def spread(seg_rows, out_weight):
    members = lax.axis_size("expert")
    n_dp = lax.axis_size("dp")
    block, width = out_weight.shape
    vmem = pl.BlockSpec(memory_space=pltpu.VMEM)
    hbm = pl.BlockSpec(memory_space=pl.ANY)
    dma = pltpu.SemaphoreType.DMA
    seg_shape = (members,) + seg_rows.shape
    return pl.pallas_call(
        spread_kernel,
        out_shape=(
            jax.ShapeDtypeStruct(seg_shape, jnp.int32),
            jax.ShapeDtypeStruct((n_dp * block, width), out_weight.dtype),
        ),
        in_specs=[vmem, vmem],
        out_specs=(vmem, hbm),
        scratch_shapes=[
            pltpu.VMEM(seg_shape, jnp.int32),
            dma, dma, dma,
            dma((n_dp,)), dma((n_dp,)), dma((n_dp,)), dma((n_dp,)),
        ],
        compiler_params=pltpu.CompilerParams(collective_id=2, has_side_effects=True),
        cost_estimate=pl.CostEstimate(flops=0, bytes_accessed=150_000_000, transcendentals=0),
        name="spread",
    )(seg_rows, out_weight)


def pages_kernel(page_ref, rows_hbm, out_ref, sems):
    count = out_ref.shape[0]
    last = rows_hbm.shape[0] // PAGE - 1
    copies = []
    for n in range(count):
        page = jnp.minimum(jnp.maximum(page_ref[n], 0), last)
        copies.append(
            pltpu.make_async_copy(
                rows_hbm.at[pl.ds(pl.multiple_of(page * PAGE, PAGE), PAGE)],
                out_ref.at[n],
                sems.at[n],
            )
        )
        copies[-1].start()
    for copy in copies:
        copy.wait()


def take_pages(pages, rows):
    count = pages.shape[0]
    return pl.pallas_call(
        pages_kernel,
        out_shape=jax.ShapeDtypeStruct((count, PAGE, rows.shape[1]), rows.dtype),
        in_specs=[
            pl.BlockSpec(memory_space=pltpu.SMEM),
            pl.BlockSpec(memory_space=pl.ANY),
        ],
        out_specs=pl.BlockSpec(memory_space=pltpu.VMEM),
        scratch_shapes=[pltpu.SemaphoreType.DMA((count,))],
        name="pages",
    )(pages, rows)


def body(
    hidden_in,
    queries,
    keys_values,
    segment_ids,
    routes,
    gate_weights,
    page_table,
    out_weight,
    norm_gain,
    expert_gate,
    expert_up,
    expert_down,
):
    tok_rows = hidden_in.shape[0]
    width = hidden_in.shape[1]
    groups = HQ // HK
    kv_width = HK * HD
    member = lax.axis_index("expert")
    first_row = member * tok_rows
    query_blocks = queries.reshape(tok_rows, HK, groups, HD)
    seg_local = segment_ids.reshape(tok_rows)
    query_pos = first_row + jnp.arange(tok_rows, dtype=jnp.int32)
    last_pos = first_row + tok_rows - 1
    slot_count = tok_rows // PAGE
    table_row = page_table.reshape(-1)
    pages_total = table_row.shape[0]
    targets = member * slot_count + jnp.arange(slot_count, dtype=jnp.int32)
    matches = (table_row[None, :] == targets[:, None]).astype(jnp.int32)
    page_of_slot = jnp.sum(matches * jnp.arange(pages_total, dtype=jnp.int32)[None, :], axis=1)
    score_scale = 1.0 / math.sqrt(HD)

    def attend_block(carried, inputs):
        running_max, running_sum, running_acc = carried
        kv_block, seg_block, block_start = inputs
        row_count = kv_block.shape[0]
        key_part = kv_block[:, :kv_width].reshape(row_count, HK, HD)
        value_part = kv_block[:, kv_width:].reshape(row_count, HK, HD)
        key_pos = block_start + jnp.arange(row_count, dtype=jnp.int32)
        allowed = (key_pos[None, :] <= query_pos[:, None]) & (
            seg_block[None, :] == seg_local[:, None]
        )
        allowed_wide = allowed[:, None, None, :]
        scores = (
            jnp.einsum("thgd,shd->thgs", query_blocks, key_part, preferred_element_type=jnp.float32)
            * score_scale
        )
        masked = jnp.where(allowed_wide, scores, neg_big)
        new_max = jnp.maximum(running_max, jnp.max(masked, axis=3))
        probabilities = jnp.where(allowed_wide, jnp.exp(masked - new_max[..., None]), 0.0)
        factor = jnp.exp(running_max - new_max)
        new_sum = running_sum * factor + jnp.sum(probabilities, axis=3)
        weighted = jnp.einsum(
            "thgs,shd->thgd",
            probabilities.astype(jnp.bfloat16),
            value_part,
            preferred_element_type=jnp.float32,
        )
        new_acc = running_acc * factor[..., None] + weighted
        return (new_max, new_sum, new_acc)

    def keep_state(carried, inputs):
        return carried

    def advance(carried, inputs):
        kv_block, seg_block, block_start = inputs
        row_count = kv_block.shape[0]
        needed = (block_start <= last_pos) & (seg_block[-1] >= seg_local[0])
        return (lax.cond(needed, attend_block, keep_state, carried, inputs), None)

    start_state = (
        jnp.full((tok_rows, HK, groups), neg_big, jnp.float32),
        jnp.zeros((tok_rows, HK, groups), jnp.float32),
        jnp.zeros((tok_rows, HK, groups, HD), jnp.float32),
    )
    softmax_state = start_state
    kv_piece = lax.all_gather(keys_values, "expert", axis=0, tiled=True)
    seg_all, weight_all = spread(jnp.broadcast_to(seg_local[None, :], (8, tok_rows)), out_weight)
    seg_piece = seg_all[:, 0, :].reshape(-1)
    piece_rows = kv_piece.shape[0]
    block_rows = math.gcd(piece_rows, 512)
    block_count = piece_rows // block_rows
    kv_steps = kv_piece.reshape(block_count, block_rows, kv_piece.shape[1])
    seg_steps = seg_piece.reshape(block_count, block_rows)
    block_starts = block_rows * jnp.arange(block_count, dtype=jnp.int32)
    softmax_state, _ = lax.scan(advance, softmax_state, (kv_steps, seg_steps, block_starts))
    cache_slots = take_pages(page_of_slot, kv_piece)
    running_max, running_sum, running_acc = softmax_state
    attended = (
        (running_acc / running_sum[..., None]).reshape(tok_rows, HQ * HD).astype(jnp.bfloat16)
    )
    projected = jnp.dot(
        attended,
        weight_all,
        preferred_element_type=jnp.float32,
    )
    residual = hidden_in.astype(jnp.float32) + projected
    normed = (
        residual
        * lax.rsqrt(jnp.mean(residual * residual, axis=1, keepdims=True) + norm_eps)
        * norm_gain
    ).astype(jnp.bfloat16)
    shares = gate_weights / jnp.sum(gate_weights, axis=1, keepdims=True)
    meta = jnp.concatenate([routes.T.astype(jnp.float32), shares.T], axis=0)
    hidden_out = moe(normed, residual, meta, expert_gate, expert_up, expert_down)
    return (hidden_out, cache_slots)


def solution(mesh):
    return jax.shard_map(
        body,
        mesh=mesh,
        in_specs=(
            P(("dp", "expert"), None),
            P(("dp", "expert"), None),
            P(("dp", "expert"), None),
            P("dp", "expert"),
            P(("dp", "expert"), None),
            P(("dp", "expert"), None),
            P("dp", None),
            P("dp", None),
            P(),
            P("expert", None, None),
            P("expert", None, None),
            P("expert", None, None),
        ),
        out_specs=(P(("dp", "expert"), None), P(("dp", "expert"), None, None)),
        check_vma=False,
    )
```
